32 devices in a mesh: leaf: 2 (over x), row: 4 (over y, core), col: 4 (over z).
Axes of the slice: x: 2, y: 2, z: 4, core: 2. Of those that a mesh axis runs over, the one named last changes fastest.
Arguments:
- leaf_front: float32 [2, 7, 4, 128, 7, 4, 128], P('leaf', None, 'row', None, None, 'col'), as said below
- leaf_pattern: int32 [2, 28, 28], P('leaf'), may hold values from 0 to 1, as said below
- parent_panel: float32 [1, 2, 7, 4, 128, 4, 128], P(None, 'leaf', None, 'row', None, 'col'), may hold values from -0.125 to 0.125
- parent_diag: float32 [1, 2, 7, 4, 128], P(None, 'leaf', None, 'row'), may hold values from 1.5 to 2.5
- parent_pattern: int32 [1, 2, 28, 28], replicated, may hold values from 0 to 1, as said below
- ext_map: int32 [1, 2, 24], replicated, may hold values from 0 to 27, as said below
Outputs:
- panels: float32 [2, 2, 7, 4, 128, 4, 128], P(None, 'leaf', None, 'row', None, 'col')
- top_update: float32 [2, 6, 4, 128, 6, 4, 128], P('leaf', None, 'row', None, None, 'col')
The draws below stay inside these ranges and needn't reach their ends.
Inputs may be any that keep to these rules, and one draw needn't show every extreme that they name: Each leaf_front[g], read as a matrix, is symmetric; every front built in the reference program is positive definite. leaf_pattern: symmetric, with every diagonal block 1. parent_pattern: symmetric, with every diagonal block 1. parent_pattern[d, n] belongs to node n at depth d+1; rows n of 2 / 2^(d+1) or more are not read. ext_map[d, n] belongs to node n at depth d; rows n of 2 / 2^d or more are not read. Along its 24 entries it rises strictly; ext_map[d, n, j] - j is the same for the 4 entries j of each aligned run of 4, never falls and lies in 0 to 4. Among the entries j of one class of j mod 4, at most two lie in one class of ext_map mod 4, and in every row some two do.
All inputs are finite; a program needn't handle non-finite values.
Results may differ from the reference program's by a relative error of at most 0.0003.
Values sent between devices are 32-bit elements; how exact they have to be, the bound alone decides.
A program may use at most 128 MiB of HBM per device.

```python
import math
import jax
import jax.numpy as jnp
import numpy as np
from jax import lax

BLOCK = 128
FRONT = 3584
PIVOTS = 512
FRONT_BLOCKS = 28
CONTRIB = 3072
CONTRIB_BLOCKS = 24
BLOCK_ROWS = 7
CONTRIB_ROWS = 6
LEVELS = 1
N_LEAF = 2
N_ROW = 4
N_COL = 4


size_table = np.array([[count_a, count_b, count_c, count_d, count_e] for count_a in range(3) for count_b in range(3) for count_c in range(3) for count_d in range(3) for count_e in range(3) if count_a + count_b + count_c + count_d + count_e == 6 and count_a + count_e <= 2], dtype=np.int32)


def draw_leaf_front(key, part):

    def draw_single(sub_key):
        random_part = jax.random.normal(sub_key, (FRONT, FRONT), jnp.float32)
        diagonal = jax.random.uniform(jax.random.fold_in(sub_key, 1), (FRONT,), jnp.float32, 0.9, 1.5)
        spread_scale = 0.35 / math.sqrt(2.0 * FRONT)
        return (random_part + random_part.T) * spread_scale + jnp.diag(diagonal)
    leaf_keys = jax.random.split(jax.random.fold_in(key, 7), N_LEAF)
    fronts = lax.map(draw_single, leaf_keys)
    return fronts.reshape(N_LEAF, BLOCK_ROWS, N_ROW, BLOCK, BLOCK_ROWS, N_COL, BLOCK)


def pattern_draw(key, leading):
    tosses = jax.random.randint(key, leading + (FRONT_BLOCKS, FRONT_BLOCKS), 0, 5, dtype=jnp.int32)
    row_ids = jnp.arange(FRONT_BLOCKS)[:, None]
    col_ids = jnp.arange(FRONT_BLOCKS)[None, :]
    lower_part = jnp.where(row_ids > col_ids, (tosses < 3).astype(jnp.int32), 0)
    return lower_part + jnp.swapaxes(lower_part, -1, -2) + (row_ids == col_ids).astype(jnp.int32)


def draw_leaf_pattern(key, part):
    return pattern_draw(jax.random.fold_in(key, 11), (N_LEAF,))


def draw_parent_pattern(key, part):
    return pattern_draw(jax.random.fold_in(key, 13), (LEVELS, N_LEAF))


def draw_ext_map(key, part):
    table = jnp.asarray(size_table)
    chosen = jax.random.randint(jax.random.fold_in(key, 17), (LEVELS, N_LEAF), 0, table.shape[0], dtype=jnp.int32)
    counts = table[chosen]
    bounds = jnp.cumsum(counts, axis=-1)
    quad_index = jnp.arange(CONTRIB_BLOCKS // N_ROW, dtype=jnp.int32)
    offsets = jnp.sum((bounds[..., None, :] <= quad_index[:, None]).astype(jnp.int32), axis=-1)
    return jnp.arange(CONTRIB_BLOCKS, dtype=jnp.int32) + jnp.repeat(offsets, N_ROW, axis=-1)


def shard_levels(rng, shape, cuts, low, high):
    factor_of = 1.0
    for axis_at, parts in cuts:
        heights = jax.random.uniform(jax.random.fold_in(jax.random.fold_in(rng, 6), axis_at), (parts,), jnp.float32, low / len(cuts), high / len(cuts))
        factor_of = factor_of * jnp.repeat(jnp.exp(heights), shape[axis_at] // parts).reshape((-1,) + (1,) * (len(shape) - 1 - axis_at))
    return factor_of


def noise(rng, dims, scale, limit, cuts=(), held_as=jnp.bfloat16):
    drawn = scale * jax.random.normal(rng, dims, jnp.float32)
    if cuts:
        drawn = drawn * shard_levels(rng, dims, cuts, -0.22, 0.18)
    return jnp.clip(drawn, -limit, limit).astype(held_as)


def setup_inputs(seed: int = 0) -> dict:
    key_list = jax.random.split(jax.random.key(seed), 7)
    return {
        "leaf_front": draw_leaf_front(jax.random.fold_in(key_list[6], 71), 0),
        "leaf_pattern": draw_leaf_pattern(jax.random.fold_in(key_list[6], 71), 0),
        "parent_panel": noise(key_list[2], (LEVELS, N_LEAF, BLOCK_ROWS, N_ROW, BLOCK, N_COL, BLOCK), (FRONT * 2 // 3) ** -0.5, 0.125, ((1, 2), (3, 4), (5, 4)), jnp.float32),
        "parent_diag": jnp.clip(1.5 + 1.0 * jax.random.uniform(key_list[3], (LEVELS, N_LEAF, BLOCK_ROWS, N_ROW, BLOCK), jnp.float32) ** shard_levels(key_list[3], (LEVELS, N_LEAF, BLOCK_ROWS, N_ROW, BLOCK), ((1, 2), (3, 4)), -0.2, 0.2), 1.5, 2.5),
        "parent_pattern": draw_parent_pattern(jax.random.fold_in(key_list[6], 71), 0),
        "ext_map": draw_ext_map(jax.random.fold_in(key_list[6], 71), 0),
    }


highest = lax.Precision.HIGHEST

def symmetric_lower(matrix):
    return jnp.tril(matrix) + jnp.swapaxes(jnp.tril(matrix, -1), -1, -2)

def partial_factor(front):
    symmetric = symmetric_lower(front)
    pivot_factor = jnp.linalg.cholesky(symmetric[:PIVOTS, :PIVOTS])
    lower_rows = lax.linalg.triangular_solve(pivot_factor, symmetric[PIVOTS:, :PIVOTS], left_side=False, lower=True, transpose_a=True)
    update = symmetric[PIVOTS:, PIVOTS:] - jnp.dot(lower_rows.astype(jnp.float32), lower_rows.T.astype(jnp.float32), precision=highest, preferred_element_type=jnp.float32)
    panel_col = jnp.concatenate([pivot_factor, lower_rows], axis=0)
    return (panel_col, update)

def block_mask(pattern):
    return jnp.repeat(jnp.repeat(pattern.astype(jnp.float32), BLOCK, axis=0), BLOCK, axis=1)

def extend_add(front, update, child_map):
    positions = (child_map[:, None] * BLOCK + jnp.arange(BLOCK, dtype=jnp.int32)[None, :]).reshape(-1).astype(jnp.int32)
    return front.at[positions[:, None], positions[None, :]].add(update)

def reference(leaf_front, leaf_pattern, parent_panel, parent_diag, parent_pattern, ext_map):
    leaves = leaf_front.reshape(N_LEAF, FRONT, FRONT)

    def leaf_step(members):
        front, pattern = members
        return partial_factor(block_mask(pattern) * front)
    panels_now, updates = lax.map(leaf_step, (leaves, leaf_pattern))
    panel_list = [panels_now]
    for depth in range(LEVELS):
        node_count = N_LEAF >> depth + 1
        group_span = 2 ** (depth + 1)
        shares = parent_panel[depth].reshape(node_count, group_span, FRONT, PIVOTS).sum(axis=1)
        diagonals = parent_diag[depth].reshape(node_count, group_span, FRONT).sum(axis=1)
        child_maps = ext_map[depth, :2 * node_count].reshape(node_count, 2, CONTRIB_BLOCKS)
        child_updates = updates.reshape(node_count, 2, CONTRIB, CONTRIB)
        patterns = parent_pattern[depth, :node_count]

        def node_step(members):
            share, diagonal, pattern, maps_here, children = members
            initials = jnp.concatenate([share, jnp.zeros((FRONT, FRONT - PIVOTS), jnp.float32)], axis=1) + jnp.diag(diagonal)
            front = block_mask(pattern) * initials
            front = extend_add(front, children[0], maps_here[0])
            front = extend_add(front, children[1], maps_here[1])
            return partial_factor(front)
        panels_now, updates = lax.map(node_step, (shares, diagonals, patterns, child_maps, child_updates))
        panel_list.append(panels_now)
    stacked = jnp.stack([jnp.repeat(panel_set, 2 ** depth, axis=0) for depth, panel_set in enumerate(panel_list)])
    panels = stacked.reshape(LEVELS + 1, N_LEAF, BLOCK_ROWS, N_ROW, BLOCK, N_COL, BLOCK)
    top_update = jnp.repeat(jnp.tril(updates), 2 ** LEVELS, axis=0).reshape(N_LEAF, CONTRIB_ROWS, N_ROW, BLOCK, CONTRIB_ROWS, N_COL, BLOCK)
    return (panels, top_update)
```

```python
import functools
import jax
import jax.numpy as jnp
from jax import lax
from jax.experimental import pallas as pl
from jax.experimental.pallas import tpu as pltpu
from jax.sharding import PartitionSpec as P

highest = lax.Precision.HIGHEST
slot_limit = 2


def from_root(value, axis, source):
    kept = jnp.where(lax.axis_index(axis) == source, value, 0).astype(value.dtype)
    return lax.psum(kept, axis)


def partner_2(block, axis, bit):
    count = lax.axis_size(axis)
    route = []
    for low in range(count):
        high = low | 1 << bit
        if high != low and high < count:
            route += [(low, high), (high, low)]
    return lax.ppermute(block, axis, route)


def symmetric_lower(matrix):
    return jnp.tril(matrix) + jnp.tril(matrix, -1).T


def local_mask(pattern, my_row, my_col, block_rows, grid_side):
    layout = pattern.reshape(block_rows, grid_side, block_rows, grid_side).astype(jnp.float32)
    picked = lax.dynamic_index_in_dim(layout, my_row, 1, keepdims=False)
    picked = lax.dynamic_index_in_dim(picked, my_col, 2, keepdims=False)
    return picked[:, None, :, None]


def eliminate_block(block):
    size = block.shape[0]
    groups = size // 8
    lane = lax.broadcasted_iota(jnp.int32, (8, size), 1)
    sub = lax.broadcasted_iota(jnp.int32, (8, size), 0)
    rows = [block[8 * g : 8 * g + 8, :] for g in range(groups)]
    for g in range(groups):
        base = 8 * g
        here = rows[g]
        inside = jnp.logical_and(lane >= base, lane < base + 8)
        line = [jnp.broadcast_to(here[a : a + 1, :], (8, size)) for a in range(8)]
        s = [
            [
                jnp.broadcast_to(line[a][:, base + b : base + b + 1], (8, size)) if b >= a else None
                for b in range(8)
            ]
            for a in range(8)
        ]
        line = [
            jnp.where(inside, jnp.where(lane == base + a, 1.0, 0.0), line[a]) for a in range(8)
        ]
        inverse = [None] * 8
        ratio = [[None] * 8 for _ in range(8)]
        for a in range(8):
            inverse[a] = 1.0 / s[a][a]
            for b in range(a + 1, 8):
                ratio[a][b] = s[a][b] * inverse[a]
            for b in range(a + 1, 8):
                for c in range(b, 8):
                    s[b][c] = s[b][c] - ratio[a][b] * s[a][c]
                line[b] = line[b] - ratio[a][b] * line[a]
        done = line[0]
        for a in range(8):
            whole = line[a]
            for b in range(a, 8):
                whole = jnp.where(lane == base + b, s[a][b], whole)
            done = whole if a == 0 else jnp.where(sub == a, whole, done)
        rows[g] = done
        if g + 1 < groups:
            solved = [None] * 8
            for a in range(7, -1, -1):
                total = line[a] * inverse[a]
                for b in range(a + 1, 8):
                    total = total - ratio[a][b] * solved[b]
                solved[a] = total
            for h in range(g + 1, groups):
                before = rows[h]
                total = jnp.where(inside, 0.0, before)
                for a in range(8):
                    spread = jnp.broadcast_to(before[:, base + a : base + a + 1], (8, size))
                    total = total - spread * solved[a]
                rows[h] = total
    return jnp.concatenate(rows, axis=0)


def pivot_kernel(block_size, corner_ref, upper_ref, inverse_ref, row_ref):
    order = corner_ref.shape[0]
    inverse_ref[...] = corner_ref[...]
    row_id = lax.broadcasted_iota(jnp.int32, (block_size, block_size), 0)
    col_id = lax.broadcasted_iota(jnp.int32, (block_size, block_size), 1)
    wide_col = lax.broadcasted_iota(jnp.int32, (block_size, order), 1)
    tall_row = lax.broadcasted_iota(jnp.int32, (order, block_size), 0)

    def step(k, carry):
        start = pl.multiple_of(k * block_size, block_size)
        here = pl.ds(start, block_size)
        reduced = eliminate_block(inverse_ref[here, here])
        pivot = jnp.sum(jnp.where(row_id == col_id, reduced, 0.0), axis=1, keepdims=True)
        scale = lax.rsqrt(pivot)
        scale = scale * (1.5 - 0.5 * pivot * scale * scale)
        scaled = reduced * scale
        small = jnp.where(row_id > col_id, scaled, jnp.where(row_id == col_id, scale, 0.0))
        row = jnp.dot(
            small, inverse_ref[here, :], precision=highest, preferred_element_type=jnp.float32
        )
        right = jnp.where(wide_col >= start + block_size, row, 0.0)
        upper_ref[here, :] = right
        upper_ref[here, here] = jnp.where(row_id <= col_id, scaled, 0.0)
        row_ref[...] = row
        row_ref[:, here] = small
        inverse_ref[:, here] = jnp.where(
            tall_row >= start + block_size, 0.0, inverse_ref[:, here]
        )
        inverse_ref[...] = inverse_ref[...] - lax.dot_general(
            right,
            row_ref[...],
            (((0,), (0,)), ((), ())),
            precision=highest,
            preferred_element_type=jnp.float32,
        )
        inverse_ref[here, :] = jnp.where(wide_col < start + block_size, row_ref[...], 0.0)
        return carry

    lax.fori_loop(0, order // block_size, step, 0)


def pivot_factors(corner, block_size):
    order = corner.shape[0]
    shape = jax.ShapeDtypeStruct((order, order), jnp.float32)
    return pl.pallas_call(
        functools.partial(pivot_kernel, block_size),
        out_shape=(shape, shape),
        in_specs=[pl.BlockSpec(memory_space=pltpu.VMEM)],
        out_specs=(pl.BlockSpec(memory_space=pltpu.VMEM),) * 2,
        scratch_shapes=[pltpu.VMEM((block_size, order), jnp.float32)],
        cost_estimate=pl.CostEstimate(
            flops=64 * order**3, bytes_accessed=64 * 4 * order * order, transcendentals=0
        ),
        name="pivot_factors",
    )(corner)


def factor_whole(front_local, my_row, my_col, grid_side, block_size, kept):
    local_order = front_local.shape[0]
    block_rows = local_order // block_size
    pivots = grid_side * block_size
    squares = lax.all_gather(
        front_local[None, :block_size, :block_size], ("row", "col"), axis=0, tiled=True
    )
    corner = (
        squares.reshape(grid_side, grid_side, block_size, block_size)
        .transpose(0, 2, 1, 3)
        .reshape(pivots, pivots)
    )
    pivot_wide = lax.all_gather(front_local[:, :block_size], "col", axis=1, tiled=True)
    upper, inverse = pivot_factors(symmetric_lower(corner), block_size)
    solved = jnp.einsum(
        "ik,jk->ij",
        pivot_wide[block_size:],
        inverse,
        precision=highest,
        preferred_element_type=jnp.float32,
    )
    top_rows = lax.dynamic_slice(upper, (0, my_row * block_size), (pivots, block_size)).T
    rows_here = jnp.concatenate([top_rows, solved], axis=0)
    rows_there = from_root(rows_here, "row", my_col)
    picked_rows = jnp.take(
        rows_there.reshape(block_rows, block_size, pivots), kept, axis=0
    ).reshape(-1, pivots)
    panel_col = lax.dynamic_slice(rows_here, (0, my_col * block_size), (local_order, block_size))
    update = front_local[block_size:, block_size:] - jnp.einsum(
        "ik,jk->ij",
        rows_here[block_size:],
        picked_rows[block_size:],
        precision=lax.Precision.HIGH,
        preferred_element_type=jnp.float32,
    )
    return (panel_col, update)


def factor(front_local, my_row, my_col, grid_side, block_size, kept):
    return factor_whole(front_local, my_row, my_col, grid_side, block_size, kept)


def pack_lower(front):
    return jnp.concatenate(
        [front[t, :, : t + 1, :].reshape(front.shape[1], -1) for t in range(front.shape[0])],
        axis=1,
    )


def unpack_lower(packed, block_rows):
    block_size = packed.shape[0]
    rows = []
    start = 0
    for t in range(block_rows):
        width = (t + 1) * block_size
        rows.append(
            jnp.pad(
                packed[:, start : start + width], ((0, 0), (0, block_rows * block_size - width))
            )
        )
        start += width
    return jnp.concatenate(rows, axis=0)


def route_tables(child_map, grid_side, my_index, block_rows):
    layout = child_map.reshape(-1, grid_side)
    row_total = layout.shape[0]
    target = layout % grid_side
    home_row = layout // grid_side
    order_ids = jnp.arange(row_total)
    before = order_ids[:, None] > order_ids[None, :]
    shared = target[:, None, :] == target[None, :, :]
    position = jnp.sum(jnp.logical_and(shared, before[:, :, None]).astype(jnp.int32), axis=1)
    own_target = lax.dynamic_index_in_dim(target, my_index, 1, keepdims=False)
    own_position = lax.dynamic_index_in_dim(position, my_index, 1, keepdims=False)
    slot_ids = jnp.arange(slot_limit)
    side_ids = jnp.arange(grid_side)
    outgoing = jnp.logical_and(
        own_target[None, None, :] == side_ids[:, None, None],
        own_position[None, None, :] == slot_ids[None, :, None],
    ).astype(jnp.int32)
    send_index = jnp.sum(outgoing * order_ids[None, None, :], axis=2).reshape(-1)
    send_valid = jnp.sum(outgoing, axis=2).reshape(-1).astype(jnp.float32)
    matches = (
        (target == my_index)[:, :, None, None]
        & (position[:, :, None, None] == slot_ids[None, None, :, None])
        & (home_row[:, :, None, None] == jnp.arange(block_rows)[None, None, None, :])
    )
    incoming = jnp.sum(matches.astype(jnp.int32), axis=0)
    flat_ids = side_ids[:, None] * slot_limit + slot_ids[None, :]
    place_index = jnp.sum(incoming * flat_ids[:, :, None], axis=(0, 1))
    place_valid = jnp.sum(incoming, axis=(0, 1)).astype(jnp.float32)
    return (send_index, send_valid, place_index, place_valid)


def shards(leaf_front, leaf_pattern, parent_panel, parent_diag, parent_pattern, ext_map):
    block_rows = leaf_front.shape[1]
    block_size = leaf_front.shape[3]
    local_order = block_rows * block_size
    contrib_rows = block_rows - 1
    levels = parent_panel.shape[0]
    grid_side = lax.axis_size("row")
    my_row = lax.axis_index("row")
    my_col = lax.axis_index("col")
    my_leaf = lax.axis_index("leaf")
    all_blocks = jnp.arange(block_rows, dtype=jnp.int32)
    leaf_local = leaf_front[0, :, 0, :, :, 0, :]
    front_local = (
        leaf_local * local_mask(leaf_pattern[0], my_row, my_col, block_rows, grid_side)
    ).reshape(local_order, local_order)
    panel_col, update = factor(front_local, my_row, my_col, grid_side, block_size, all_blocks)
    panel_list = [panel_col]
    acc_panel = parent_panel.reshape(levels, block_rows, block_size, block_size)
    acc_diag = parent_diag.reshape(levels, block_rows, block_size)
    block_same = (
        jnp.arange(block_rows)[:, None, None, None] == jnp.arange(block_rows)[None, None, :, None]
    )
    element_same = (
        jnp.arange(block_size)[None, :, None, None] == jnp.arange(block_size)[None, None, None, :]
    )
    diag_spots = jnp.logical_and(jnp.logical_and(block_same, element_same), my_row == my_col)
    for depth in range(levels):
        child_node = jnp.right_shift(my_leaf, depth)
        child_map = lax.dynamic_index_in_dim(ext_map[depth], child_node, 0, keepdims=False)
        row_src, row_ok, row_place, row_in = route_tables(child_map, grid_side, my_row, block_rows)
        col_src, col_ok, col_place, col_in = route_tables(child_map, grid_side, my_col, block_rows)
        update_blocks = update.reshape(contrib_rows, block_size, contrib_rows, block_size)
        rows_taken = jnp.take(update_blocks, row_src, axis=0) * row_ok[:, None, None, None]
        packed = jnp.take(rows_taken, col_src, axis=2) * col_ok[None, None, :, None]
        packed = packed.reshape(
            grid_side, slot_limit, block_size, grid_side, slot_limit, block_size
        )
        packed = packed.transpose(0, 3, 1, 4, 2, 5).reshape(
            grid_side * grid_side, slot_limit * slot_limit, block_size, block_size
        )
        received = lax.all_to_all(packed, ("row", "col"), split_axis=0, concat_axis=0, tiled=True)
        received = received.reshape(
            grid_side, grid_side, slot_limit, slot_limit, block_size, block_size
        )
        received = received.transpose(0, 2, 1, 3, 4, 5).reshape(
            grid_side * slot_limit, grid_side * slot_limit, block_size, block_size
        )
        placed = jnp.take(received, row_place, axis=0)
        placed = jnp.take(placed, col_place, axis=1)
        placed = placed * (row_in[:, None, None, None] * col_in[None, :, None, None])
        spread = placed.transpose(0, 2, 1, 3)
        parent_node = jnp.right_shift(my_leaf, depth + 1)
        pattern = lax.dynamic_index_in_dim(parent_pattern[depth], parent_node, 0, keepdims=False)
        mask_here = local_mask(pattern, my_row, my_col, block_rows, grid_side)
        own_front = spread + jnp.where(
            diag_spots, acc_diag[depth][:, :, None, None] * mask_here, 0.0
        )
        own_front = own_front.at[:, :, 0, :].add(mask_here[:, :, 0, :] * acc_panel[depth])
        if depth + 1 < levels:
            partner, partner_panel, partner_diag = partner_2(
                (pack_lower(own_front), acc_panel[depth + 1 :], acc_diag[depth + 1 :]),
                "leaf",
                depth,
            )
            acc_panel = jnp.concatenate(
                [acc_panel[: depth + 1], acc_panel[depth + 1 :] + partner_panel], axis=0
            )
            acc_diag = jnp.concatenate(
                [acc_diag[: depth + 1], acc_diag[depth + 1 :] + partner_diag], axis=0
            )
        else:
            partner = partner_2(pack_lower(own_front), "leaf", depth)
        front_local = own_front.reshape(local_order, local_order) + unpack_lower(
            partner, block_rows
        )
        panel_col, update = factor(front_local, my_row, my_col, grid_side, block_size, all_blocks)
        panel_list.append(panel_col)
    panels = jnp.stack(panel_list).reshape(levels + 1, 1, block_rows, 1, block_size, 1, block_size)
    element_ids = jnp.arange(block_size)
    row_ids = (grid_side * (jnp.arange(contrib_rows) + 1) + my_row)[
        :, None
    ] * block_size + element_ids[None, :]
    col_ids = (grid_side * (jnp.arange(contrib_rows) + 1) + my_col)[
        :, None
    ] * block_size + element_ids[None, :]
    keep_lower = row_ids[:, :, None, None] >= col_ids[None, None, :, :]
    top_rows = jnp.where(
        keep_lower, update.reshape(contrib_rows, block_size, contrib_rows, block_size), 0.0
    )
    top_update = top_rows.reshape(1, contrib_rows, 1, block_size, contrib_rows, 1, block_size)
    return (panels, top_update)


def solution(mesh):
    return jax.shard_map(
        shards,
        mesh=mesh,
        in_specs=(
            P("leaf", None, "row", None, None, "col", None),
            P("leaf", None, None),
            P(None, "leaf", None, "row", None, "col", None),
            P(None, "leaf", None, "row", None),
            P(),
            P(),
        ),
        out_specs=(
            P(None, "leaf", None, "row", None, "col", None),
            P("leaf", None, "row", None, None, "col", None),
        ),
        check_vma=False,
    )
```

```python
import functools
import jax
import jax.numpy as jnp
from jax import lax
from jax.experimental import pallas as pl
from jax.experimental.pallas import tpu as pltpu
from jax.sharding import PartitionSpec as P

highest = lax.Precision.HIGHEST
slot_limit = 2


def from_root(value, axis, source):
    kept = jnp.where(lax.axis_index(axis) == source, value, 0).astype(value.dtype)
    return lax.psum(kept, axis)


def partner_2(block, axis, bit):
    count = lax.axis_size(axis)
    route = []
    for low in range(count):
        high = low | 1 << bit
        if high != low and high < count:
            route += [(low, high), (high, low)]
    return lax.ppermute(block, axis, route)


def symmetric_lower(matrix):
    return jnp.tril(matrix) + jnp.tril(matrix, -1).T


def local_mask(pattern, my_row, my_col, block_rows, grid_side):
    layout = pattern.reshape(block_rows, grid_side, block_rows, grid_side).astype(jnp.float32)
    picked = lax.dynamic_index_in_dim(layout, my_row, 1, keepdims=False)
    picked = lax.dynamic_index_in_dim(picked, my_col, 2, keepdims=False)
    return picked[:, None, :, None]


def eliminate_block(block):
    size = block.shape[0]
    groups = size // 8
    lane = lax.broadcasted_iota(jnp.int32, (8, size), 1)
    sub = lax.broadcasted_iota(jnp.int32, (8, size), 0)
    rows = [block[8 * g : 8 * g + 8, :] for g in range(groups)]
    for g in range(groups):
        base = 8 * g
        here = rows[g]
        inside = jnp.logical_and(lane >= base, lane < base + 8)
        line = [jnp.broadcast_to(here[a : a + 1, :], (8, size)) for a in range(8)]
        s = [
            [
                jnp.broadcast_to(line[a][:, base + b : base + b + 1], (8, size)) if b >= a else None
                for b in range(8)
            ]
            for a in range(8)
        ]
        line = [
            jnp.where(inside, jnp.where(lane == base + a, 1.0, 0.0), line[a]) for a in range(8)
        ]
        inverse = [None] * 8
        ratio = [[None] * 8 for _ in range(8)]
        for a in range(8):
            inverse[a] = 1.0 / s[a][a]
            for b in range(a + 1, 8):
                ratio[a][b] = s[a][b] * inverse[a]
            for b in range(a + 1, 8):
                for c in range(b, 8):
                    s[b][c] = s[b][c] - ratio[a][b] * s[a][c]
                line[b] = line[b] - ratio[a][b] * line[a]
        done = line[0]
        for a in range(8):
            whole = line[a]
            for b in range(a, 8):
                whole = jnp.where(lane == base + b, s[a][b], whole)
            done = whole if a == 0 else jnp.where(sub == a, whole, done)
        rows[g] = done
        if g + 1 < groups:
            solved = [None] * 8
            for a in range(7, -1, -1):
                total = line[a] * inverse[a]
                for b in range(a + 1, 8):
                    total = total - ratio[a][b] * solved[b]
                solved[a] = total
            for h in range(g + 1, groups):
                before = rows[h]
                total = jnp.where(inside, 0.0, before)
                for a in range(8):
                    spread = jnp.broadcast_to(before[:, base + a : base + a + 1], (8, size))
                    total = total - spread * solved[a]
                rows[h] = total
    return jnp.concatenate(rows, axis=0)


def pivot_kernel(block_size, corner_ref, upper_ref, inverse_ref, row_ref):
    order = corner_ref.shape[0]
    inverse_ref[...] = corner_ref[...]
    row_id = lax.broadcasted_iota(jnp.int32, (block_size, block_size), 0)
    col_id = lax.broadcasted_iota(jnp.int32, (block_size, block_size), 1)
    wide_col = lax.broadcasted_iota(jnp.int32, (block_size, order), 1)
    tall_row = lax.broadcasted_iota(jnp.int32, (order, block_size), 0)

    def step(k, carry):
        start = pl.multiple_of(k * block_size, block_size)
        here = pl.ds(start, block_size)
        reduced = eliminate_block(inverse_ref[here, here])
        pivot = jnp.sum(jnp.where(row_id == col_id, reduced, 0.0), axis=1, keepdims=True)
        scale = lax.rsqrt(pivot)
        scale = scale * (1.5 - 0.5 * pivot * scale * scale)
        scaled = reduced * scale
        small = jnp.where(row_id > col_id, scaled, jnp.where(row_id == col_id, scale, 0.0))
        row = jnp.dot(
            small, inverse_ref[here, :], precision=highest, preferred_element_type=jnp.float32
        )
        right = jnp.where(wide_col >= start + block_size, row, 0.0)
        upper_ref[here, :] = right
        upper_ref[here, here] = jnp.where(row_id <= col_id, scaled, 0.0)
        row_ref[...] = row
        row_ref[:, here] = small
        inverse_ref[:, here] = jnp.where(
            tall_row >= start + block_size, 0.0, inverse_ref[:, here]
        )
        inverse_ref[...] = inverse_ref[...] - lax.dot_general(
            right,
            row_ref[...],
            (((0,), (0,)), ((), ())),
            precision=highest,
            preferred_element_type=jnp.float32,
        )
        inverse_ref[here, :] = jnp.where(wide_col < start + block_size, row_ref[...], 0.0)
        return carry

    lax.fori_loop(0, order // block_size, step, 0)


def pivot_factors(corner, block_size):
    order = corner.shape[0]
    shape = jax.ShapeDtypeStruct((order, order), jnp.float32)
    return pl.pallas_call(
        functools.partial(pivot_kernel, block_size),
        out_shape=(shape, shape),
        in_specs=[pl.BlockSpec(memory_space=pltpu.VMEM)],
        out_specs=(pl.BlockSpec(memory_space=pltpu.VMEM),) * 2,
        scratch_shapes=[pltpu.VMEM((block_size, order), jnp.float32)],
        cost_estimate=pl.CostEstimate(
            flops=64 * order**3, bytes_accessed=64 * 4 * order * order, transcendentals=0
        ),
        name="pivot_factors",
    )(corner)


def rows_times(left, right, precision=highest):
    return jnp.einsum(
        "ik,jk->ij", left, right, precision=precision, preferred_element_type=jnp.float32
    )


def gather_corner(front_local, grid_side, block_size):
    pivots = grid_side * block_size
    squares = lax.all_gather(
        front_local[None, :block_size, :block_size], ("row", "col"), axis=0, tiled=True
    )
    return (
        squares.reshape(grid_side, grid_side, block_size, block_size)
        .transpose(0, 2, 1, 3)
        .reshape(pivots, pivots)
    )


def top_block(upper, my_row, my_col, block_size):
    start = (my_col * block_size, my_row * block_size)
    block = lax.dynamic_slice(upper, (start[1], start[0]), (block_size, block_size))
    flipped = lax.dynamic_slice(upper, start, (block_size, block_size)).T
    return jnp.where(my_row >= my_col, flipped, jnp.zeros_like(block))


def factor_top(front_local, my_row, my_col, grid_side, block_size):
    corner = gather_corner(front_local, grid_side, block_size)
    wide = lax.all_gather(front_local[block_size:, :block_size], "col", axis=1, tiled=True)
    upper, inverse = pivot_factors(symmetric_lower(corner), block_size)
    rows_here = rows_times(wide, inverse)
    rows_there = from_root(rows_here, "row", my_col)
    own = lax.dynamic_slice(
        rows_here, (0, my_col * block_size), (rows_here.shape[0], block_size)
    )
    panel_col = jnp.concatenate([top_block(upper, my_row, my_col, block_size), own], axis=0)
    update = front_local[block_size:, block_size:] - rows_times(
        rows_here, rows_there, lax.Precision.HIGH
    )
    return (panel_col, update)


def factor_child(front_local, my_row, my_col, grid_side, block_size, row_table, col_table):
    local_order = front_local.shape[0]
    block_rows = local_order // block_size
    contrib_rows = block_rows - 1
    row_src, row_ok, row_place, row_in = row_table
    col_src, col_ok, col_place, col_in = col_table
    corner = gather_corner(front_local, grid_side, block_size)
    left = front_local[block_size:, :block_size].reshape(contrib_rows, block_size, block_size)
    packed_left = jnp.take(left, row_src, axis=0) * row_ok[:, None, None]
    received_left = lax.all_to_all(
        packed_left.reshape(grid_side, slot_limit, block_size, block_size),
        "row",
        split_axis=0,
        concat_axis=0,
        tiled=True,
    ).reshape(grid_side * slot_limit, block_size, block_size)
    placed_left = jnp.take(received_left, row_place, axis=0) * row_in[:, None, None]
    wide = lax.all_gather(
        jnp.concatenate([left, placed_left], axis=0).reshape(-1, block_size),
        "col",
        axis=1,
        tiled=True,
    )
    own_wide = wide[: contrib_rows * block_size]
    placed_wide = wide[contrib_rows * block_size :]
    there_wide = from_root(placed_wide, "row", my_col)
    blocks = front_local[block_size:, block_size:].reshape(
        contrib_rows, block_size, contrib_rows, block_size
    )
    packed = jnp.take(blocks.transpose(0, 2, 1, 3), row_src, axis=0)
    packed = jnp.take(packed, col_src, axis=1)
    packed = packed * (row_ok[:, None] * col_ok[None, :])[:, :, None, None]
    packed = packed.reshape(
        grid_side, slot_limit, grid_side, slot_limit, block_size, block_size
    )
    packed = packed.transpose(0, 2, 1, 3, 4, 5).reshape(
        grid_side * grid_side, slot_limit * slot_limit, block_size, block_size
    )
    received = lax.all_to_all(packed, ("row", "col"), split_axis=0, concat_axis=0, tiled=True)
    received = received.reshape(
        grid_side, grid_side, slot_limit, slot_limit, block_size, block_size
    )
    received = received.transpose(0, 2, 1, 3, 4, 5).reshape(
        grid_side * slot_limit, grid_side * slot_limit, block_size, block_size
    )
    placed = jnp.take(received, row_place, axis=0)
    placed = jnp.take(placed, col_place, axis=1)
    placed = placed * (row_in[:, None] * col_in[None, :])[:, :, None, None]
    spread = placed.transpose(0, 2, 1, 3).reshape(local_order, local_order)
    upper, inverse = pivot_factors(symmetric_lower(corner), block_size)
    own_inverse = lax.dynamic_slice(
        inverse, (my_col * block_size, 0), (block_size, inverse.shape[1])
    )
    panel_col = jnp.concatenate(
        [top_block(upper, my_row, my_col, block_size), rows_times(own_wide, own_inverse)], axis=0
    )
    moved = spread - rows_times(
        rows_times(placed_wide, inverse),
        rows_times(there_wide, inverse),
        lax.Precision.HIGH,
    )
    return (panel_col, moved.reshape(block_rows, block_size, block_rows, block_size))


def pack_lower(front):
    return jnp.concatenate(
        [front[t, :, : t + 1, :].reshape(front.shape[1], -1) for t in range(front.shape[0])],
        axis=1,
    )


def unpack_lower(packed, block_rows):
    block_size = packed.shape[0]
    rows = []
    start = 0
    for t in range(block_rows):
        width = (t + 1) * block_size
        rows.append(
            jnp.pad(
                packed[:, start : start + width], ((0, 0), (0, block_rows * block_size - width))
            )
        )
        start += width
    return jnp.concatenate(rows, axis=0)


def route_tables(child_map, grid_side, my_index, block_rows):
    layout = child_map.reshape(-1, grid_side)
    row_total = layout.shape[0]
    target = layout % grid_side
    home_row = layout // grid_side
    order_ids = jnp.arange(row_total)
    before = order_ids[:, None] > order_ids[None, :]
    shared = target[:, None, :] == target[None, :, :]
    position = jnp.sum(jnp.logical_and(shared, before[:, :, None]).astype(jnp.int32), axis=1)
    own_target = lax.dynamic_index_in_dim(target, my_index, 1, keepdims=False)
    own_position = lax.dynamic_index_in_dim(position, my_index, 1, keepdims=False)
    slot_ids = jnp.arange(slot_limit)
    side_ids = jnp.arange(grid_side)
    outgoing = jnp.logical_and(
        own_target[None, None, :] == side_ids[:, None, None],
        own_position[None, None, :] == slot_ids[None, :, None],
    ).astype(jnp.int32)
    send_index = jnp.sum(outgoing * order_ids[None, None, :], axis=2).reshape(-1)
    send_valid = jnp.sum(outgoing, axis=2).reshape(-1).astype(jnp.float32)
    matches = (
        (target == my_index)[:, :, None, None]
        & (position[:, :, None, None] == slot_ids[None, None, :, None])
        & (home_row[:, :, None, None] == jnp.arange(block_rows)[None, None, None, :])
    )
    incoming = jnp.sum(matches.astype(jnp.int32), axis=0)
    flat_ids = side_ids[:, None] * slot_limit + slot_ids[None, :]
    place_index = jnp.sum(incoming * flat_ids[:, :, None], axis=(0, 1))
    place_valid = jnp.sum(incoming, axis=(0, 1)).astype(jnp.float32)
    return (send_index, send_valid, place_index, place_valid)


def shards(leaf_front, leaf_pattern, parent_panel, parent_diag, parent_pattern, ext_map):
    block_rows = leaf_front.shape[1]
    block_size = leaf_front.shape[3]
    local_order = block_rows * block_size
    contrib_rows = block_rows - 1
    levels = parent_panel.shape[0]
    grid_side = lax.axis_size("row")
    my_row = lax.axis_index("row")
    my_col = lax.axis_index("col")
    my_leaf = lax.axis_index("leaf")
    leaf_local = leaf_front[0, :, 0, :, :, 0, :]
    front_local = (
        leaf_local * local_mask(leaf_pattern[0], my_row, my_col, block_rows, grid_side)
    ).reshape(local_order, local_order)
    panel_list = []
    acc_panel = parent_panel.reshape(levels, block_rows, block_size, block_size)
    acc_diag = parent_diag.reshape(levels, block_rows, block_size)
    block_same = (
        jnp.arange(block_rows)[:, None, None, None] == jnp.arange(block_rows)[None, None, :, None]
    )
    element_same = (
        jnp.arange(block_size)[None, :, None, None] == jnp.arange(block_size)[None, None, None, :]
    )
    diag_spots = jnp.logical_and(jnp.logical_and(block_same, element_same), my_row == my_col)
    for depth in range(levels):
        child_node = jnp.right_shift(my_leaf, depth)
        child_map = lax.dynamic_index_in_dim(ext_map[depth], child_node, 0, keepdims=False)
        row_src, row_ok, row_place, row_in = route_tables(child_map, grid_side, my_row, block_rows)
        col_src, col_ok, col_place, col_in = route_tables(child_map, grid_side, my_col, block_rows)
        panel_col, spread = factor_child(
            front_local,
            my_row,
            my_col,
            grid_side,
            block_size,
            (row_src, row_ok, row_place, row_in),
            (col_src, col_ok, col_place, col_in),
        )
        panel_list.append(panel_col)
        parent_node = jnp.right_shift(my_leaf, depth + 1)
        pattern = lax.dynamic_index_in_dim(parent_pattern[depth], parent_node, 0, keepdims=False)
        mask_here = local_mask(pattern, my_row, my_col, block_rows, grid_side)
        own_front = spread + jnp.where(
            diag_spots, acc_diag[depth][:, :, None, None] * mask_here, 0.0
        )
        own_front = own_front.at[:, :, 0, :].add(mask_here[:, :, 0, :] * acc_panel[depth])
        if depth + 1 < levels:
            partner, partner_panel, partner_diag = partner_2(
                (pack_lower(own_front), acc_panel[depth + 1 :], acc_diag[depth + 1 :]),
                "leaf",
                depth,
            )
            acc_panel = jnp.concatenate(
                [acc_panel[: depth + 1], acc_panel[depth + 1 :] + partner_panel], axis=0
            )
            acc_diag = jnp.concatenate(
                [acc_diag[: depth + 1], acc_diag[depth + 1 :] + partner_diag], axis=0
            )
        else:
            partner = partner_2(pack_lower(own_front), "leaf", depth)
        front_local = own_front.reshape(local_order, local_order) + unpack_lower(
            partner, block_rows
        )
    panel_col, update = factor_top(front_local, my_row, my_col, grid_side, block_size)
    panel_list.append(panel_col)
    panels = jnp.stack(panel_list).reshape(levels + 1, 1, block_rows, 1, block_size, 1, block_size)
    element_ids = jnp.arange(block_size)
    row_ids = (grid_side * (jnp.arange(contrib_rows) + 1) + my_row)[
        :, None
    ] * block_size + element_ids[None, :]
    col_ids = (grid_side * (jnp.arange(contrib_rows) + 1) + my_col)[
        :, None
    ] * block_size + element_ids[None, :]
    keep_lower = row_ids[:, :, None, None] >= col_ids[None, None, :, :]
    top_rows = jnp.where(
        keep_lower, update.reshape(contrib_rows, block_size, contrib_rows, block_size), 0.0
    )
    top_update = top_rows.reshape(1, contrib_rows, 1, block_size, contrib_rows, 1, block_size)
    return (panels, top_update)


def solution(mesh):
    return jax.shard_map(
        shards,
        mesh=mesh,
        in_specs=(
            P("leaf", None, "row", None, None, "col", None),
            P("leaf", None, None),
            P(None, "leaf", None, "row", None, "col", None),
            P(None, "leaf", None, "row", None),
            P(),
            P(),
        ),
        out_specs=(
            P(None, "leaf", None, "row", None, "col", None),
            P("leaf", None, "row", None, None, "col", None),
        ),
        check_vma=False,
    )
```

```python
import functools
import jax
import jax.numpy as jnp
from jax import lax
from jax.experimental import pallas as pl
from jax.experimental.pallas import tpu as pltpu
from jax.sharding import PartitionSpec as P

highest = lax.Precision.HIGHEST
slot_limit = 2


def from_root(value, axis, source):
    kept = jnp.where(lax.axis_index(axis) == source, value, 0).astype(value.dtype)
    return lax.psum(kept, axis)


def partner_2(block, axis, bit):
    count = lax.axis_size(axis)
    route = []
    for low in range(count):
        high = low | 1 << bit
        if high != low and high < count:
            route += [(low, high), (high, low)]
    return lax.ppermute(block, axis, route)


def symmetric_lower(matrix):
    return jnp.tril(matrix) + jnp.tril(matrix, -1).T


def local_mask(pattern, my_row, my_col, block_rows, grid_side):
    layout = pattern.reshape(block_rows, grid_side, block_rows, grid_side).astype(jnp.float32)
    picked = lax.dynamic_index_in_dim(layout, my_row, 1, keepdims=False)
    picked = lax.dynamic_index_in_dim(picked, my_col, 2, keepdims=False)
    return picked[:, None, :, None]


def eliminate_block(block):
    size = block.shape[0]
    groups = size // 8
    lane = lax.broadcasted_iota(jnp.int32, (8, size), 1)
    sub = lax.broadcasted_iota(jnp.int32, (8, size), 0)
    rows = [block[8 * g : 8 * g + 8, :] for g in range(groups)]
    for g in range(groups):
        base = 8 * g
        here = rows[g]
        inside = jnp.logical_and(lane >= base, lane < base + 8)
        line = [jnp.broadcast_to(here[a : a + 1, :], (8, size)) for a in range(8)]
        s = [
            [
                jnp.broadcast_to(line[a][:, base + b : base + b + 1], (8, size)) if b >= a else None
                for b in range(8)
            ]
            for a in range(8)
        ]
        line = [
            jnp.where(inside, jnp.where(lane == base + a, 1.0, 0.0), line[a]) for a in range(8)
        ]
        inverse = [None] * 8
        ratio = [[None] * 8 for _ in range(8)]
        for a in range(8):
            inverse[a] = 1.0 / s[a][a]
            for b in range(a + 1, 8):
                ratio[a][b] = s[a][b] * inverse[a]
            for b in range(a + 1, 8):
                for c in range(b, 8):
                    s[b][c] = s[b][c] - ratio[a][b] * s[a][c]
                line[b] = line[b] - ratio[a][b] * line[a]
        done = line[0]
        for a in range(8):
            whole = line[a]
            for b in range(a, 8):
                whole = jnp.where(lane == base + b, s[a][b], whole)
            done = whole if a == 0 else jnp.where(sub == a, whole, done)
        rows[g] = done
        if g + 1 < groups:
            solved = [None] * 8
            for a in range(7, -1, -1):
                total = line[a] * inverse[a]
                for b in range(a + 1, 8):
                    total = total - ratio[a][b] * solved[b]
                solved[a] = total
            for h in range(g + 1, groups):
                before = rows[h]
                total = jnp.where(inside, 0.0, before)
                for a in range(8):
                    spread = jnp.broadcast_to(before[:, base + a : base + a + 1], (8, size))
                    total = total - spread * solved[a]
                rows[h] = total
    return jnp.concatenate(rows, axis=0)


def pivot_kernel(block_size, corner_ref, upper_ref, inverse_ref, row_ref):
    order = corner_ref.shape[0]
    inverse_ref[...] = corner_ref[...]
    row_id = lax.broadcasted_iota(jnp.int32, (block_size, block_size), 0)
    col_id = lax.broadcasted_iota(jnp.int32, (block_size, block_size), 1)
    wide_col = lax.broadcasted_iota(jnp.int32, (block_size, order), 1)
    tall_row = lax.broadcasted_iota(jnp.int32, (order, block_size), 0)

    def step(k, carry):
        start = pl.multiple_of(k * block_size, block_size)
        here = pl.ds(start, block_size)
        reduced = eliminate_block(inverse_ref[here, here])
        pivot = jnp.sum(jnp.where(row_id == col_id, reduced, 0.0), axis=1, keepdims=True)
        scale = lax.rsqrt(pivot)
        scale = scale * (1.5 - 0.5 * pivot * scale * scale)
        scaled = reduced * scale
        small = jnp.where(row_id > col_id, scaled, jnp.where(row_id == col_id, scale, 0.0))
        row = jnp.dot(
            small, inverse_ref[here, :], precision=highest, preferred_element_type=jnp.float32
        )
        right = jnp.where(wide_col >= start + block_size, row, 0.0)
        upper_ref[here, :] = right
        upper_ref[here, here] = jnp.where(row_id <= col_id, scaled, 0.0)
        row_ref[...] = row
        row_ref[:, here] = small
        inverse_ref[:, here] = jnp.where(
            tall_row >= start + block_size, 0.0, inverse_ref[:, here]
        )
        inverse_ref[...] = inverse_ref[...] - lax.dot_general(
            right,
            row_ref[...],
            (((0,), (0,)), ((), ())),
            precision=highest,
            preferred_element_type=jnp.float32,
        )
        inverse_ref[here, :] = jnp.where(wide_col < start + block_size, row_ref[...], 0.0)
        return carry

    lax.fori_loop(0, order // block_size, step, 0)


def pivot_factors(corner, block_size):
    order = corner.shape[0]
    shape = jax.ShapeDtypeStruct((order, order), jnp.float32)
    return pl.pallas_call(
        functools.partial(pivot_kernel, block_size),
        out_shape=(shape, shape),
        in_specs=[pl.BlockSpec(memory_space=pltpu.VMEM)],
        out_specs=(pl.BlockSpec(memory_space=pltpu.VMEM),) * 2,
        scratch_shapes=[pltpu.VMEM((block_size, order), jnp.float32)],
        cost_estimate=pl.CostEstimate(
            flops=64 * order**3, bytes_accessed=64 * 4 * order * order, transcendentals=0
        ),
        name="pivot_factors",
    )(corner)


def rows_times(left, right, precision=highest):
    return jnp.einsum(
        "ik,jk->ij", left, right, precision=precision, preferred_element_type=jnp.float32
    )


def gather_corner(front_local, grid_side, block_size):
    pivots = grid_side * block_size
    squares = lax.all_gather(
        front_local[None, :block_size, :block_size], ("row", "col"), axis=0, tiled=True
    )
    return (
        squares.reshape(grid_side, grid_side, block_size, block_size)
        .transpose(0, 2, 1, 3)
        .reshape(pivots, pivots)
    )


def top_block(upper, my_row, my_col, block_size):
    start = (my_col * block_size, my_row * block_size)
    block = lax.dynamic_slice(upper, (start[1], start[0]), (block_size, block_size))
    flipped = lax.dynamic_slice(upper, start, (block_size, block_size)).T
    return jnp.where(my_row >= my_col, flipped, jnp.zeros_like(block))


def factor_top(front_local, my_row, my_col, grid_side, block_size):
    corner = gather_corner(front_local, grid_side, block_size)
    wide = lax.all_gather(front_local[block_size:, :block_size], "col", axis=1, tiled=True)
    upper, inverse = pivot_factors(symmetric_lower(corner), block_size)
    rows_here = rows_times(wide, inverse)
    rows_there = from_root(rows_here, "row", my_col)
    own = lax.dynamic_slice(
        rows_here, (0, my_col * block_size), (rows_here.shape[0], block_size)
    )
    panel_col = jnp.concatenate([top_block(upper, my_row, my_col, block_size), own], axis=0)
    update = front_local[block_size:, block_size:] - rows_times(
        rows_here, rows_there, lax.Precision.HIGH
    )
    return (panel_col, update)


def factor_child(front_local, my_row, my_col, grid_side, block_size, row_table, col_table):
    local_order = front_local.shape[0]
    block_rows = local_order // block_size
    contrib_rows = block_rows - 1
    row_src, row_ok, row_place, row_in = row_table
    col_src, col_ok, col_place, col_in = col_table
    corner = gather_corner(front_local, grid_side, block_size)
    left = front_local[block_size:, :block_size].reshape(contrib_rows, block_size, block_size)
    own_wide = lax.all_gather(left.reshape(-1, block_size), "col", axis=1, tiled=True)
    pivots = own_wide.shape[1]
    packed_wide = jnp.take(
        own_wide.reshape(contrib_rows, block_size, pivots), row_src, axis=0
    ) * row_ok[:, None, None]
    packed_wide = packed_wide.reshape(grid_side, slot_limit, block_size, pivots)
    arrived = []
    for hop in range(grid_side):
        leaving = lax.dynamic_index_in_dim(
            packed_wide, (my_row + hop) % grid_side, 0, keepdims=False
        )
        if hop:
            route = [(low, (low + hop) % grid_side) for low in range(grid_side)]
            leaving = lax.ppermute(leaving, "row", route)
        arrived.append(leaving)
    hop_place = ((my_row - row_place // slot_limit) % grid_side) * slot_limit
    hop_place = hop_place + row_place % slot_limit
    placed_wide = (
        jnp.take(jnp.concatenate(arrived, axis=0), hop_place, axis=0) * row_in[:, None, None]
    )
    placed_wide = placed_wide.reshape(local_order, pivots)
    there_wide = from_root(placed_wide, "row", my_col)
    blocks = front_local[block_size:, block_size:].reshape(
        contrib_rows, block_size, contrib_rows, block_size
    )
    packed = jnp.take(blocks.transpose(0, 2, 1, 3), row_src, axis=0)
    packed = jnp.take(packed, col_src, axis=1)
    packed = packed * (row_ok[:, None] * col_ok[None, :])[:, :, None, None]
    packed = packed.reshape(
        grid_side, slot_limit, grid_side, slot_limit, block_size, block_size
    )
    packed = packed.transpose(0, 2, 1, 3, 4, 5).reshape(
        grid_side * grid_side, slot_limit * slot_limit, block_size, block_size
    )
    received = lax.all_to_all(packed, ("row", "col"), split_axis=0, concat_axis=0, tiled=True)
    received = received.reshape(
        grid_side, grid_side, slot_limit, slot_limit, block_size, block_size
    )
    received = received.transpose(0, 2, 1, 3, 4, 5).reshape(
        grid_side * slot_limit, grid_side * slot_limit, block_size, block_size
    )
    placed = jnp.take(received, row_place, axis=0)
    placed = jnp.take(placed, col_place, axis=1)
    placed = placed * (row_in[:, None] * col_in[None, :])[:, :, None, None]
    spread = placed.transpose(0, 2, 1, 3).reshape(local_order, local_order)
    upper, inverse = pivot_factors(symmetric_lower(corner), block_size)
    own_inverse = lax.dynamic_slice(
        inverse, (my_col * block_size, 0), (block_size, inverse.shape[1])
    )
    panel_col = jnp.concatenate(
        [top_block(upper, my_row, my_col, block_size), rows_times(own_wide, own_inverse)], axis=0
    )
    moved = spread - rows_times(
        rows_times(placed_wide, inverse),
        rows_times(there_wide, inverse),
        lax.Precision.HIGH,
    )
    return (panel_col, moved)


def pack_lower(front, block_size):
    pieces = [
        front[start : start + block_size, : start + block_size]
        for start in range(0, front.shape[0], block_size)
    ]
    return jnp.concatenate(pieces, axis=1)


def unpack_lower(packed, block_rows):
    block_size = packed.shape[0]
    rows = []
    start = 0
    for t in range(block_rows):
        width = (t + 1) * block_size
        rows.append(
            jnp.pad(
                packed[:, start : start + width], ((0, 0), (0, block_rows * block_size - width))
            )
        )
        start += width
    return jnp.concatenate(rows, axis=0)


def route_tables(child_map, grid_side, my_index, block_rows):
    layout = child_map.reshape(-1, grid_side)
    row_total = layout.shape[0]
    target = layout % grid_side
    home_row = layout // grid_side
    order_ids = jnp.arange(row_total)
    before = order_ids[:, None] > order_ids[None, :]
    shared = target[:, None, :] == target[None, :, :]
    position = jnp.sum(jnp.logical_and(shared, before[:, :, None]).astype(jnp.int32), axis=1)
    own_target = lax.dynamic_index_in_dim(target, my_index, 1, keepdims=False)
    own_position = lax.dynamic_index_in_dim(position, my_index, 1, keepdims=False)
    slot_ids = jnp.arange(slot_limit)
    side_ids = jnp.arange(grid_side)
    outgoing = jnp.logical_and(
        own_target[None, None, :] == side_ids[:, None, None],
        own_position[None, None, :] == slot_ids[None, :, None],
    ).astype(jnp.int32)
    send_index = jnp.sum(outgoing * order_ids[None, None, :], axis=2).reshape(-1)
    send_valid = jnp.sum(outgoing, axis=2).reshape(-1).astype(jnp.float32)
    matches = (
        (target == my_index)[:, :, None, None]
        & (position[:, :, None, None] == slot_ids[None, None, :, None])
        & (home_row[:, :, None, None] == jnp.arange(block_rows)[None, None, None, :])
    )
    incoming = jnp.sum(matches.astype(jnp.int32), axis=0)
    flat_ids = side_ids[:, None] * slot_limit + slot_ids[None, :]
    place_index = jnp.sum(incoming * flat_ids[:, :, None], axis=(0, 1))
    place_valid = jnp.sum(incoming, axis=(0, 1)).astype(jnp.float32)
    return (send_index, send_valid, place_index, place_valid)


def shards(leaf_front, leaf_pattern, parent_panel, parent_diag, parent_pattern, ext_map):
    block_rows = leaf_front.shape[1]
    block_size = leaf_front.shape[3]
    local_order = block_rows * block_size
    contrib_rows = block_rows - 1
    levels = parent_panel.shape[0]
    grid_side = lax.axis_size("row")
    my_row = lax.axis_index("row")
    my_col = lax.axis_index("col")
    my_leaf = lax.axis_index("leaf")
    leaf_local = leaf_front[0, :, 0, :, :, 0, :]
    front_local = (
        leaf_local * local_mask(leaf_pattern[0], my_row, my_col, block_rows, grid_side)
    ).reshape(local_order, local_order)
    panel_list = []
    acc_panel = parent_panel.reshape(levels, block_rows, block_size, block_size)
    acc_diag = parent_diag.reshape(levels, block_rows, block_size)
    order_ids = jnp.arange(local_order)
    diag_spots = jnp.logical_and(order_ids[:, None] == order_ids[None, :], my_row == my_col)
    for depth in range(levels):
        child_node = jnp.right_shift(my_leaf, depth)
        child_map = lax.dynamic_index_in_dim(ext_map[depth], child_node, 0, keepdims=False)
        row_src, row_ok, row_place, row_in = route_tables(child_map, grid_side, my_row, block_rows)
        col_src, col_ok, col_place, col_in = route_tables(child_map, grid_side, my_col, block_rows)
        panel_col, spread = factor_child(
            front_local,
            my_row,
            my_col,
            grid_side,
            block_size,
            (row_src, row_ok, row_place, row_in),
            (col_src, col_ok, col_place, col_in),
        )
        panel_list.append(panel_col)
        parent_node = jnp.right_shift(my_leaf, depth + 1)
        pattern = lax.dynamic_index_in_dim(parent_pattern[depth], parent_node, 0, keepdims=False)
        mask_here = local_mask(pattern, my_row, my_col, block_rows, grid_side)
        mask_diag = jnp.repeat(jnp.diagonal(mask_here[:, 0, :, 0]), block_size)
        mask_left = jnp.repeat(mask_here[:, 0, 0, 0], block_size)
        own_front = spread + jnp.where(
            diag_spots, (acc_diag[depth].reshape(-1) * mask_diag)[:, None], 0.0
        )
        own_left = own_front[:, :block_size] + mask_left[:, None] * acc_panel[depth].reshape(
            local_order, block_size
        )
        own_front = jnp.concatenate([own_left, own_front[:, block_size:]], axis=1)
        if depth + 1 < levels:
            partner, partner_panel, partner_diag = partner_2(
                (pack_lower(own_front, block_size), acc_panel[depth + 1 :], acc_diag[depth + 1 :]),
                "leaf",
                depth,
            )
            acc_panel = jnp.concatenate(
                [acc_panel[: depth + 1], acc_panel[depth + 1 :] + partner_panel], axis=0
            )
            acc_diag = jnp.concatenate(
                [acc_diag[: depth + 1], acc_diag[depth + 1 :] + partner_diag], axis=0
            )
        else:
            partner = partner_2(pack_lower(own_front, block_size), "leaf", depth)
        front_local = own_front + unpack_lower(
            partner, block_rows
        )
    panel_col, update = factor_top(front_local, my_row, my_col, grid_side, block_size)
    panel_list.append(panel_col)
    panels = jnp.stack(panel_list).reshape(levels + 1, 1, block_rows, 1, block_size, 1, block_size)
    element_ids = jnp.arange(block_size)
    row_ids = (grid_side * (jnp.arange(contrib_rows) + 1) + my_row)[
        :, None
    ] * block_size + element_ids[None, :]
    col_ids = (grid_side * (jnp.arange(contrib_rows) + 1) + my_col)[
        :, None
    ] * block_size + element_ids[None, :]
    keep_lower = row_ids[:, :, None, None] >= col_ids[None, None, :, :]
    top_rows = jnp.where(
        keep_lower, update.reshape(contrib_rows, block_size, contrib_rows, block_size), 0.0
    )
    top_update = top_rows.reshape(1, contrib_rows, 1, block_size, contrib_rows, 1, block_size)
    return (panels, top_update)


def solution(mesh):
    return jax.shard_map(
        shards,
        mesh=mesh,
        in_specs=(
            P("leaf", None, "row", None, None, "col", None),
            P("leaf", None, None),
            P(None, "leaf", None, "row", None, "col", None),
            P(None, "leaf", None, "row", None),
            P(),
            P(),
        ),
        out_specs=(
            P(None, "leaf", None, "row", None, "col", None),
            P("leaf", None, "row", None, None, "col", None),
        ),
        check_vma=False,
    )
```
